512 devices in a mesh: seq: 64 (over x, z), head: 8 (over y, core).
Axes of the slice: x: 4, y: 4, z: 16, core: 2. Of those that a mesh axis runs over, the one named last changes fastest.
Arguments:
- queries: bfloat16 [32768, 4096], P('seq', 'head'), may hold values from -6 to 6
- keys: bfloat16 [32768, 4096], P('seq', 'head'), may hold values from -0.5390625 to 0.5390625
- values: bfloat16 [32768, 4096], P('seq', 'head'), may hold values from -6 to 6
- log_decay: float32 [32, 32768], P('head', 'seq'), may hold values from -1 to 0, as said below
- out_weight: bfloat16 [4096, 3072], P('head'), may hold values from -0.125 to 0.125
Outputs:
- layer_out: bfloat16 [32768, 3072], P('seq', 'head')
The draws below stay inside these ranges and needn't reach their ends.
Inputs may be any that keep to these rules, and one draw needn't show every extreme that they name: log_decay is negative.
All inputs are finite; a program needn't handle non-finite values.
Results may differ from the reference program's by a relative error of at most 0.018.
Values may be sent and summed in bfloat16 or wider, within the bound.
A program may use at most 64 MiB of HBM per device.

```python
import math
import jax
import jax.numpy as jnp
from jax import lax

HEADS = 32
HEAD_DIM = 128
OUT = 3072
TOK_DEV = 512
TOKEN_POSITIONS = 32768
FEAT = 4096
N_HEAD = 8


def draw_log_decay(key, part):
    key_rows_full = jax.random.split(jax.random.fold_in(key, 17), 7)
    fast_share = 0.5
    fast_heads = jax.random.uniform(key_rows_full[0], (HEADS,)) < fast_share
    fast_rate = -jax.random.uniform(key_rows_full[1], (HEADS,), minval=1.0 / 50.0, maxval=1.0 / 30.0)
    block_loss = jnp.exp(jax.random.uniform(key_rows_full[2], (HEADS,), minval=math.log(0.05), maxval=math.log(0.3)))
    slow_rate = -block_loss / TOK_DEV
    baseline_decay_rate = jnp.where(fast_heads, fast_rate, slow_rate)
    blocks = TOKEN_POSITIONS // TOK_DEV
    block_multiplier = jnp.exp(jax.random.uniform(key_rows_full[3], (HEADS, blocks), minval=math.log(0.7), maxval=math.log(1.4)))
    block_multiplier = jnp.repeat(block_multiplier, TOK_DEV, axis=1)
    decay_jitter = jax.random.uniform(key_rows_full[4], (HEADS, TOKEN_POSITIONS), minval=0.5, maxval=1.5)
    spike_token_positions = jax.random.randint(key_rows_full[5], (2,), 0, TOKEN_POSITIONS)
    spike_fraction = jax.random.uniform(key_rows_full[6], (2,), minval=0.2, maxval=0.4)
    token_places = jnp.arange(TOKEN_POSITIONS)
    spike_log_decay = jnp.sum((token_places[None, :] == spike_token_positions[:, None]).astype(jnp.float32) * jnp.log(1.0 - spike_fraction)[:, None], axis=0)
    return (baseline_decay_rate[:, None] * block_multiplier * decay_jitter + spike_log_decay[None, :]).astype(jnp.float32)


def spiked(entries, stream_key, source, target, shards_of, factor):
    def block_of(position):
        return (jnp.arange(entries.shape[position]) // (entries.shape[position] // shards_of)).reshape((-1,) + (1,) * (entries.ndim - 1 - position))

    one_side = jax.random.permutation(stream_key, shards_of)[block_of(target)]
    other_side = (block_of(target) + shards_of // 2) % shards_of
    return jnp.where((block_of(source) == one_side) | (block_of(source) == other_side), factor * entries, entries)


def shard_levels(own_key, shape, pieces, low, top_value):
    def one(position, blocks):
        heights = jax.random.uniform(jax.random.fold_in(jax.random.fold_in(own_key, 6), position), (blocks,), jnp.float32, low / len(pieces), top_value / len(pieces))
        return jnp.repeat(jnp.exp(heights), shape[position] // blocks).reshape((-1,) + (1,) * (len(shape) - position - 1))

    level = one(*pieces[0])
    for cut in pieces[1:]:
        level = level * one(*cut)
    return level


def gaussian(own_key, dims, spread, reach, shards=(), kind=jnp.bfloat16):
    result = jax.random.normal(own_key, dims, jnp.float32) * spread
    if len(shards) > 0:
        result = shard_levels(own_key, dims, shards, -0.22, 0.18) * result
    return jnp.clip(result, min=-reach, max=reach).astype(kind)


def heavy_noise(rng, dims, scale, limit, pieces, heavy, held_as=jnp.bfloat16):
    entries = scale * jax.random.normal(rng, dims, jnp.float32)
    if pieces:
        entries = entries * shard_levels(rng, dims, pieces, -0.22, 0.18)
    return jnp.clip(spiked(entries, jax.random.fold_in(rng, 3), *heavy), -limit, limit).astype(held_as)


def setup_inputs(seed: int = 0) -> dict:
    arg_keys = jax.random.split(jax.random.key(seed), 6)
    return {
        "queries": gaussian(arg_keys[0], (TOKEN_POSITIONS, FEAT), 1.0, 6.0, ((0, 64), (1, 8))),
        "keys": gaussian(arg_keys[1], (TOKEN_POSITIONS, FEAT), 0.09, 0.5390625, ((0, 64), (1, 8))),
        "values": gaussian(arg_keys[2], (TOKEN_POSITIONS, FEAT), 1.0, 6.0, ((0, 64), (1, 8))),
        "log_decay": draw_log_decay(jax.random.fold_in(arg_keys[5], 71), 0),
        "out_weight": heavy_noise(arg_keys[4], (FEAT, OUT), FEAT ** -0.5, 0.125, ((0, 8),), (0, 1, 8, 2.0)),
    }


def reference(queries, keys, values, log_decay, out_weight):
    blocks = TOKEN_POSITIONS // TOK_DEV
    group_width = FEAT // N_HEAD
    query_all = queries.reshape(blocks, TOK_DEV, HEADS, HEAD_DIM)
    key_all = keys.reshape(blocks, TOK_DEV, HEADS, HEAD_DIM)
    value_all = values.reshape(blocks, TOK_DEV, HEADS, HEAD_DIM)
    decay_all = log_decay.reshape(HEADS, blocks, TOK_DEV).transpose(1, 0, 2)
    causal_mask = jnp.tril(jnp.ones((TOK_DEV, TOK_DEV), dtype=bool))

    def block_step(carry_state, inputs_block):
        q_block, k_block, v_block, g_block = inputs_block
        cumulative = jnp.cumsum(g_block, axis=1)
        scores = jnp.einsum('thd,shd->hts', q_block.astype(jnp.float32), k_block.astype(jnp.float32))
        log_gaps = jnp.where(causal_mask[None], cumulative[:, :, None] - cumulative[:, None, :], 0.0)
        gaps = jnp.where(causal_mask[None], jnp.exp(log_gaps), 0.0)
        weighted = (scores * gaps).astype(jnp.bfloat16)
        intra_term = jnp.einsum('hts,shd->thd', weighted.astype(jnp.float32), v_block.astype(jnp.float32))
        query_scaled = q_block.astype(jnp.float32) * jnp.exp(cumulative).T[:, :, None]
        inter_term = jnp.einsum('thd,hde->the', query_scaled, carry_state, precision=lax.Precision.HIGHEST)
        mixed_out = intra_term + inter_term
        normed = (mixed_out * lax.rsqrt(lax.optimization_barrier(jnp.mean(mixed_out * mixed_out, axis=-1, keepdims=True)) + 1e-05)).astype(jnp.bfloat16)
        block_decay = cumulative[:, -1]
        scaled_keys = (k_block.astype(jnp.float32) * jnp.exp(block_decay[:, None] - cumulative).T[:, :, None]).astype(jnp.bfloat16)
        moments = jnp.einsum('thd,the->hde', scaled_keys.astype(jnp.float32), v_block.astype(jnp.float32))
        carry_state = carry_state * jnp.exp(block_decay)[:, None, None] + moments
        return (carry_state, normed)
    start_state = jnp.zeros((HEADS, HEAD_DIM, HEAD_DIM), jnp.float32)
    final_state, normed_all = lax.scan(block_step, start_state, (query_all, key_all, value_all, decay_all))
    grouped = normed_all.reshape(TOKEN_POSITIONS, N_HEAD, group_width).transpose(1, 0, 2)
    weight_groups = out_weight.reshape(N_HEAD, group_width, OUT)

    def group_step(running, inputs_group):
        features, weight_rows = inputs_group
        group_part = jnp.dot(features, weight_rows, preferred_element_type=jnp.float32)
        group_part = lax.optimization_barrier(group_part.astype(jnp.bfloat16)).astype(jnp.float32)
        return (running + group_part, None)
    running, unused = lax.scan(group_step, jnp.zeros((TOKEN_POSITIONS, OUT), jnp.float32), (grouped, weight_groups))
    return running.astype(jnp.bfloat16)
```

```python
import functools

import jax
import jax.numpy as jnp
from jax import lax
from jax.experimental import pallas as pl
from jax.experimental.pallas import tpu as pltpu
from jax.sharding import PartitionSpec as P

MESH = pl.DeviceIdType.MESH
F32, BF16 = jnp.float32, jnp.bfloat16


def far_first(n):
    return sorted(range(1, n), key=lambda k: (-min(k, n - k), k))


def kernel(
    xs, zs, ys,
    q_ref, k_ref, v_ref, g_ref, w_ref, out_ref,
    mom_out, mom_in, pref, pref_decay, tot_out, tot_in, car_out, car_in,
    intra, grown, normed, pair_out, pair_in, mine, ring_out, ring_in,
    s_mom, r_mom, s_tot, r_tot, s_car, r_car, s_pair, r_pair, s_ring, r_ring,
):
    seq, head = lax.axis_index("seq"), lax.axis_index("head")
    x, z = lax.div(seq, zs), lax.rem(seq, zs)
    y, c = lax.div(head, 2), lax.rem(head, 2)
    heads, toks = g_ref.shape
    dim = q_ref.shape[1] // heads
    rows = heads * dim // zs
    per = dim // rows
    cols = out_ref.shape[1]
    half = toks // 2

    def z_peer(k):
        return (x * zs + lax.rem(z + k, zs), head)

    def x_peer(k):
        return (lax.rem(x + k, xs) * zs + z, head)

    def y_peer(k):
        return (seq, lax.rem(y + k, ys) * 2 + c)

    partner = (seq, y * 2 + 1 - c)

    barrier = pltpu.get_barrier_semaphore()
    peers = [z_peer(k) for k in far_first(zs)] + [x_peer(k) for k in far_first(xs)]
    peers += [partner, y_peer(1), y_peer(ys - 1)]
    for peer in peers:
        pl.semaphore_signal(barrier, inc=1, device_id=peer, device_id_type=MESH)

    g = g_ref[...]
    low = lax.broadcasted_iota(jnp.int32, (toks, toks), 0) >= lax.broadcasted_iota(
        jnp.int32, (toks, toks), 1
    )
    tri = low.astype(F32)
    cum_row = lax.dot_general(
        g, tri, (((1,), (1,)), ((), ())), precision=lax.Precision.HIGHEST,
        preferred_element_type=F32,
    )
    cum_col = cum_row.T
    grown[...] = jnp.exp(cum_col)

    for h in range(heads):
        lanes = slice(h * dim, (h + 1) * dim)
        col = cum_col[:, h : h + 1]
        end = cum_col[toks - 1 : toks, h : h + 1]
        scaled = (k_ref[:, lanes].astype(F32) * jnp.exp(end - col)).astype(BF16)
        moments = lax.dot_general(
            scaled, v_ref[:, lanes], (((0,), (0,)), ((), ())), preferred_element_type=F32
        )
        decay = jnp.broadcast_to(jnp.exp(end), (8, dim))
        coarse = decay.astype(BF16).astype(F32)
        tile = jnp.concatenate([coarse, decay - coarse], axis=0).astype(BF16)
        for p in range(per):
            mom_out[h * per + p, 0:rows, :] = moments[p * rows : (p + 1) * rows].astype(BF16)
            mom_out[h * per + p, rows : rows + 16, :] = tile

    pl.semaphore_wait(barrier, len(peers))

    mom_copies = []
    for k in far_first(zs):
        mom_copies.append(
            pltpu.make_async_remote_copy(
                src_ref=mom_out.at[lax.rem(z + k, zs)], dst_ref=mom_in.at[z],
                send_sem=s_mom.at[k], recv_sem=r_mom.at[k],
                device_id=z_peer(k), device_id_type=MESH,
            )
        )
        mom_copies[-1].start()
    mom_in[z] = mom_out[z]

    def within(h):
        lanes = slice(h * dim, (h + 1) * dim)
        scores = lax.dot_general(
            q_ref[:, lanes], k_ref[:, lanes], (((1,), (1,)), ((), ())),
            preferred_element_type=F32,
        )
        gap = cum_col[:, h : h + 1] - cum_row[h : h + 1, :]
        weighted = (scores * jnp.exp(jnp.where(low, gap, -jnp.inf))).astype(BF16)
        intra[:, lanes] = jnp.dot(weighted, v_ref[:, lanes], preferred_element_type=F32)

    for h in range(heads // 2):
        within(h)

    for copy in mom_copies:
        copy.wait_recv()

    state = jnp.zeros((rows, dim), F32)
    decay = jnp.ones((8, dim), F32)
    for j in range(zs):
        pref[j] = state
        pref_decay[j] = decay
        step = mom_in[j, rows : rows + 16, :].astype(F32)
        step = step[0:8] + step[8:16]
        state = state * step[0:1] + mom_in[j, 0:rows, :].astype(F32)
        decay = decay * step
    tot_out[0:rows, :] = state
    tot_out[rows : rows + 8, :] = decay
    tot_copies = []
    for k in far_first(xs):
        tot_copies.append(
            pltpu.make_async_remote_copy(
                src_ref=tot_out, dst_ref=tot_in.at[x],
                send_sem=s_tot.at[k], recv_sem=r_tot.at[k],
                device_id=x_peer(k), device_id_type=MESH,
            )
        )
        tot_copies[-1].start()
    tot_in[x] = tot_out[...]
    for copy in tot_copies:
        copy.wait_recv()

    before = jnp.zeros((rows, dim), F32)
    for j in range(xs):
        new = before * tot_in[j, rows : rows + 1, :] + tot_in[j, 0:rows, :]
        before = jnp.where(j < x, new, before)
    for j in range(zs):
        car_out[j] = (pref[j] + pref_decay[j, 0:1, :] * before).astype(BF16)
    car_copies = []
    for k in far_first(zs):
        car_copies.append(
            pltpu.make_async_remote_copy(
                src_ref=car_out.at[lax.rem(z + k, zs)], dst_ref=car_in.at[z],
                send_sem=s_car.at[k], recv_sem=r_car.at[k],
                device_id=z_peer(k), device_id_type=MESH,
            )
        )
        car_copies[-1].start()
    car_in[z] = car_out[z]

    for h in range(heads // 2, heads):
        within(h)

    for copy in car_copies:
        copy.wait_recv()

    for h in range(heads):
        lanes = slice(h * dim, (h + 1) * dim)
        carried = car_in[h * per : (h + 1) * per].reshape(dim, dim)
        inter = jnp.dot(q_ref[:, lanes], carried, preferred_element_type=F32)
        mixed = intra[:, lanes] + inter * grown[:, h : h + 1]
        scale = lax.rsqrt(jnp.mean(mixed * mixed, axis=-1, keepdims=True) + 1e-05)
        normed[:, lanes] = (mixed * scale).astype(BF16)

    def project(to_y, to_c):
        start = pl.multiple_of((to_y * 2 + to_c) * cols, 128)
        return jnp.dot(
            normed[...], w_ref[:, pl.ds(start, cols)], preferred_element_type=F32
        ).astype(BF16)

    order = (2, 1, 3, 0)
    pair_copies = {}
    for o in order:
        pair_out[o] = project(lax.rem(y + o, ys), 1 - c)
        pair_copies[o] = pltpu.make_async_remote_copy(
            src_ref=pair_out.at[o], dst_ref=pair_in.at[o],
            send_sem=s_pair.at[o], recv_sem=r_pair.at[o],
            device_id=partner, device_id_type=MESH,
        )
        pair_copies[o].start()

    def ring(slot, source, k):
        copy = pltpu.make_async_remote_copy(
            src_ref=source, dst_ref=ring_in.at[slot],
            send_sem=s_ring.at[slot], recv_sem=r_ring.at[slot],
            device_id=y_peer(k), device_id_type=MESH,
        )
        copy.start()
        return copy

    top, bottom = slice(0, half), slice(half, toks)
    copies = [None] * 6
    for o in order:
        own = project(lax.rem(y + o, ys), c).astype(F32)
        pair_copies[o].wait_recv()
        both = own + pair_in[o].astype(F32)
        mine[o] = both.astype(BF16)
        if o == 2:
            copies[0] = ring(0, mine.at[2, pl.ds(0, half)], 1)
            copies[1] = ring(1, mine.at[2, pl.ds(half, half)], ys - 1)
        elif o == 1:
            copies[2] = ring(2, mine.at[1, pl.ds(half, half)], 1)
        elif o == 3:
            copies[3] = ring(3, mine.at[3, pl.ds(0, half)], ys - 1)
    copies[0].wait_recv()
    ring_out[0] = (mine[1, top, :].astype(F32) + ring_in[0].astype(F32)).astype(BF16)
    copies[4] = ring(4, ring_out.at[0], 1)
    copies[1].wait_recv()
    ring_out[1] = (mine[3, bottom, :].astype(F32) + ring_in[1].astype(F32)).astype(BF16)
    copies[5] = ring(5, ring_out.at[1], ys - 1)
    copies[2].wait_recv()
    copies[3].wait_recv()
    copies[4].wait_recv()
    out_ref[top, :] = (
        mine[0, top, :].astype(F32) + ring_in[3].astype(F32) + ring_in[4].astype(F32)
    ).astype(BF16)
    copies[5].wait_recv()
    out_ref[bottom, :] = (
        mine[0, bottom, :].astype(F32) + ring_in[2].astype(F32) + ring_in[5].astype(F32)
    ).astype(BF16)

    for copy in mom_copies + tot_copies + car_copies + list(pair_copies.values()) + copies:
        copy.wait_send()


def on_device(xs, zs, ys, queries, keys, values, log_decay, out_weight):
    heads, toks = log_decay.shape
    feat = queries.shape[1]
    dim = feat // heads
    rows = feat // zs
    cols = out_weight.shape[1] // (ys * 2)
    vmem = pl.BlockSpec(memory_space=pltpu.VMEM)
    dma = pltpu.SemaphoreType.DMA
    return pl.pallas_call(
        functools.partial(kernel, xs, zs, ys),
        out_shape=jax.ShapeDtypeStruct((toks, cols), BF16),
        in_specs=[vmem] * 5,
        out_specs=vmem,
        scratch_shapes=[
            pltpu.VMEM((zs, rows + 16, dim), BF16),
            pltpu.VMEM((zs, rows + 16, dim), BF16),
            pltpu.VMEM((zs, rows, dim), F32),
            pltpu.VMEM((zs, 8, dim), F32),
            pltpu.VMEM((rows + 8, dim), F32),
            pltpu.VMEM((xs, rows + 8, dim), F32),
            pltpu.VMEM((zs, rows, dim), BF16),
            pltpu.VMEM((zs, rows, dim), BF16),
            pltpu.VMEM((toks, feat), F32),
            pltpu.VMEM((toks, heads), F32),
            pltpu.VMEM((toks, feat), BF16),
            pltpu.VMEM((ys, toks, cols), BF16),
            pltpu.VMEM((ys, toks, cols), BF16),
            pltpu.VMEM((ys, toks, cols), BF16),
            pltpu.VMEM((2, toks // 2, cols), BF16),
            pltpu.VMEM((6, toks // 2, cols), BF16),
            dma((zs,)), dma((zs,)), dma((xs,)), dma((xs,)), dma((zs,)), dma((zs,)),
            dma((ys,)), dma((ys,)), dma((6,)), dma((6,)),
        ],
        compiler_params=pltpu.CompilerParams(
            collective_id=0, has_side_effects=True, vmem_limit_bytes=60 * 1024 * 1024
        ),
    )(queries, keys, values, log_decay, out_weight)


def solution(mesh, xs=4):
    zs = mesh.shape["seq"] // xs
    ys = mesh.shape["head"] // 2
    return jax.shard_map(
        functools.partial(on_device, xs, zs, ys),
        mesh=mesh,
        in_specs=(
            P("seq", "head"),
            P("seq", "head"),
            P("seq", "head"),
            P("head", "seq"),
            P("head", None),
        ),
        out_specs=P("seq", "head"),
        check_vma=False,
    )
```

```python
import functools

import jax
import jax.numpy as jnp
from jax import lax
from jax.experimental import pallas as pl
from jax.experimental.pallas import tpu as pltpu
from jax.sharding import PartitionSpec as P

MESH = pl.DeviceIdType.MESH
F32, BF16 = jnp.float32, jnp.bfloat16


def far_first(n):
    return sorted(range(1, n), key=lambda k: (-min(k, n - k), k))


def kernel(
    xs, zs, ys,
    q_hbm, k_hbm, v_hbm, g_hbm, w_hbm, out_ref,
    q_ref, k_ref, v_ref, g_ref, w_ref,
    mom_out, mom_in, dec_out, dec_in, pref, pref_decay,
    tot_out, tot_in, end_out, end_in, car_out, car_in,
    intra, grown, normed, pair_out, pair_in, mine, ring_out, ring_in,
    s_mom, r_mom, s_dec, r_dec, s_tot, r_tot, s_end, r_end, s_car, r_car,
    s_pair, r_pair, s_ring, r_ring, s_load,
):
    seq, head = lax.axis_index("seq"), lax.axis_index("head")
    x, z = lax.div(seq, zs), lax.rem(seq, zs)
    y, c = lax.div(head, 2), lax.rem(head, 2)
    heads, toks = g_ref.shape
    dim = q_ref.shape[1] // heads
    rows = heads * dim // zs
    per = dim // rows
    cols = out_ref.shape[1]
    half = toks // 2

    def z_peer(k):
        return (x * zs + lax.rem(z + k, zs), head)

    def x_peer(k):
        return (lax.rem(x + k, xs) * zs + z, head)

    def y_peer(k):
        return (seq, lax.rem(y + k, ys) * 2 + c)

    partner = (seq, y * 2 + 1 - c)

    barrier = pltpu.get_barrier_semaphore()
    peers = [z_peer(k) for k in far_first(zs)] + [x_peer(k) for k in far_first(xs)]
    peers += [partner, y_peer(1), y_peer(ys - 1)]
    for peer in peers:
        pl.semaphore_signal(barrier, inc=1, device_id=peer, device_id_type=MESH)

    loads = []
    for n, (source, target) in enumerate(
        ((g_hbm, g_ref), (k_hbm, k_ref), (v_hbm, v_ref), (q_hbm, q_ref), (w_hbm, w_ref))
    ):
        loads.append(pltpu.make_async_copy(source, target, s_load.at[n]))
        loads[-1].start()

    loads[0].wait()
    g = g_ref[...]
    low = lax.broadcasted_iota(jnp.int32, (toks, toks), 0) >= lax.broadcasted_iota(
        jnp.int32, (toks, toks), 1
    )
    tri = low.astype(F32)
    cum_row = lax.dot_general(
        g, tri, (((1,), (1,)), ((), ())), precision=lax.Precision.HIGHEST,
        preferred_element_type=F32,
    )
    cum_col = cum_row.T
    grown[...] = jnp.exp(cum_col)

    loads[1].wait()
    loads[2].wait()
    for h in range(heads):
        lanes = slice(h * dim, (h + 1) * dim)
        col = cum_col[:, h : h + 1]
        end = cum_col[toks - 1 : toks, h : h + 1]
        scaled = (k_ref[:, lanes].astype(F32) * jnp.exp(end - col)).astype(BF16)
        moments = lax.dot_general(
            scaled, v_ref[:, lanes], (((0,), (0,)), ((), ())), preferred_element_type=F32
        )
        dec_out[h] = jnp.broadcast_to(jnp.exp(end), (1, dim))
        for p in range(per):
            mom_out[h * per + p] = moments[p * rows : (p + 1) * rows].astype(BF16)

    pl.semaphore_wait(barrier, len(peers))

    mom_copies = []
    for k in far_first(zs):
        mom_copies.append(
            pltpu.make_async_remote_copy(
                src_ref=mom_out.at[lax.rem(z + k, zs)], dst_ref=mom_in.at[z],
                send_sem=s_mom.at[k], recv_sem=r_mom.at[k],
                device_id=z_peer(k), device_id_type=MESH,
            )
        )
        mom_copies[-1].start()
        mom_copies.append(
            pltpu.make_async_remote_copy(
                src_ref=dec_out.at[lax.div(lax.rem(z + k, zs), per)], dst_ref=dec_in.at[z],
                send_sem=s_dec.at[k], recv_sem=r_dec.at[k],
                device_id=z_peer(k), device_id_type=MESH,
            )
        )
        mom_copies[-1].start()
    mom_in[z] = mom_out[z]
    dec_in[z] = dec_out[lax.div(z, per)]
    loads[3].wait()

    def within(h):
        lanes = slice(h * dim, (h + 1) * dim)
        scores = lax.dot_general(
            q_ref[:, lanes], k_ref[:, lanes], (((1,), (1,)), ((), ())),
            preferred_element_type=F32,
        )
        gap = cum_col[:, h : h + 1] - cum_row[h : h + 1, :]
        weighted = (scores * jnp.exp(jnp.where(low, gap, -jnp.inf))).astype(BF16)
        intra[:, lanes] = jnp.dot(weighted, v_ref[:, lanes], preferred_element_type=F32)

    for h in range(heads // 2):
        within(h)

    for copy in mom_copies:
        copy.wait_recv()

    state = jnp.zeros((rows, dim), F32)
    decay = jnp.ones((1, dim), F32)
    for j in range(zs):
        pref[j] = state
        pref_decay[j] = decay
        state = state * dec_in[j] + mom_in[j].astype(F32)
        decay = decay * dec_in[j]
    tot_out[...] = state.astype(BF16)
    end_out[...] = decay
    tot_copies = []
    for k in far_first(xs):
        tot_copies.append(
            pltpu.make_async_remote_copy(
                src_ref=tot_out, dst_ref=tot_in.at[x],
                send_sem=s_tot.at[k], recv_sem=r_tot.at[k],
                device_id=x_peer(k), device_id_type=MESH,
            )
        )
        tot_copies[-1].start()
        tot_copies.append(
            pltpu.make_async_remote_copy(
                src_ref=end_out, dst_ref=end_in.at[x],
                send_sem=s_end.at[k], recv_sem=r_end.at[k],
                device_id=x_peer(k), device_id_type=MESH,
            )
        )
        tot_copies[-1].start()
    tot_in[x] = tot_out[...]
    end_in[x] = end_out[...]
    for copy in tot_copies:
        copy.wait_recv()

    before = jnp.zeros((rows, dim), F32)
    for j in range(xs):
        new = before * end_in[j] + tot_in[j].astype(F32)
        before = jnp.where(j < x, new, before)
    for j in range(zs):
        car_out[j] = (pref[j] + pref_decay[j] * before).astype(BF16)
    car_copies = []
    for k in far_first(zs):
        car_copies.append(
            pltpu.make_async_remote_copy(
                src_ref=car_out.at[lax.rem(z + k, zs)], dst_ref=car_in.at[z],
                send_sem=s_car.at[k], recv_sem=r_car.at[k],
                device_id=z_peer(k), device_id_type=MESH,
            )
        )
        car_copies[-1].start()
    car_in[z] = car_out[z]

    for h in range(heads // 2, heads):
        within(h)

    for copy in car_copies:
        copy.wait_recv()

    for h in range(heads):
        lanes = slice(h * dim, (h + 1) * dim)
        carried = car_in[h * per : (h + 1) * per].reshape(dim, dim)
        inter = jnp.dot(q_ref[:, lanes], carried, preferred_element_type=F32)
        mixed = intra[:, lanes] + inter * grown[:, h : h + 1]
        scale = lax.rsqrt(jnp.mean(mixed * mixed, axis=-1, keepdims=True) + 1e-05)
        normed[:, lanes] = (mixed * scale).astype(BF16)

    def project(to_y, to_c):
        start = pl.multiple_of((to_y * 2 + to_c) * cols, 128)
        return jnp.dot(
            normed[...], w_ref[:, pl.ds(start, cols)], preferred_element_type=F32
        ).astype(BF16)

    loads[4].wait()
    pair_copies = {}

    def give(o):
        pair_out[o] = project(lax.rem(y + o, ys), 1 - c)
        pair_copies[o] = pltpu.make_async_remote_copy(
            src_ref=pair_out.at[o], dst_ref=pair_in.at[o],
            send_sem=s_pair.at[o], recv_sem=r_pair.at[o],
            device_id=partner, device_id_type=MESH,
        )
        pair_copies[o].start()

    def keep(o):
        own = project(lax.rem(y + o, ys), c).astype(F32)
        pair_copies[o].wait_recv()
        mine[o] = (own + pair_in[o].astype(F32)).astype(BF16)

    def ring(slot, source, k):
        copy = pltpu.make_async_remote_copy(
            src_ref=source, dst_ref=ring_in.at[slot],
            send_sem=s_ring.at[slot], recv_sem=r_ring.at[slot],
            device_id=y_peer(k), device_id_type=MESH,
        )
        copy.start()
        return copy

    top, bottom = slice(0, half), slice(half, toks)
    copies = [None] * 6
    give(2)
    give(1)
    keep(2)
    copies[0] = ring(0, mine.at[2, pl.ds(0, half)], 1)
    copies[1] = ring(1, mine.at[2, pl.ds(half, half)], ys - 1)
    give(3)
    keep(1)
    copies[2] = ring(2, mine.at[1, pl.ds(half, half)], 1)
    give(0)
    keep(3)
    copies[3] = ring(3, mine.at[3, pl.ds(0, half)], ys - 1)
    keep(0)
    copies[0].wait_recv()
    ring_out[0] = (mine[1, top, :].astype(F32) + ring_in[0].astype(F32)).astype(BF16)
    copies[4] = ring(4, ring_out.at[0], 1)
    copies[1].wait_recv()
    ring_out[1] = (mine[3, bottom, :].astype(F32) + ring_in[1].astype(F32)).astype(BF16)
    copies[5] = ring(5, ring_out.at[1], ys - 1)
    copies[2].wait_recv()
    copies[3].wait_recv()
    copies[4].wait_recv()
    out_ref[top, :] = (
        mine[0, top, :].astype(F32) + ring_in[3].astype(F32) + ring_in[4].astype(F32)
    ).astype(BF16)
    copies[5].wait_recv()
    out_ref[bottom, :] = (
        mine[0, bottom, :].astype(F32) + ring_in[2].astype(F32) + ring_in[5].astype(F32)
    ).astype(BF16)

    for copy in mom_copies + tot_copies + car_copies + list(pair_copies.values()) + copies:
        copy.wait_send()


def on_device(xs, zs, ys, queries, keys, values, log_decay, out_weight):
    heads, toks = log_decay.shape
    feat = queries.shape[1]
    dim = feat // heads
    rows = feat // zs
    cols = out_weight.shape[1] // (ys * 2)
    vmem = pl.BlockSpec(memory_space=pltpu.VMEM)
    dma = pltpu.SemaphoreType.DMA
    return pl.pallas_call(
        functools.partial(kernel, xs, zs, ys),
        out_shape=jax.ShapeDtypeStruct((toks, cols), BF16),
        in_specs=[pl.BlockSpec(memory_space=pl.ANY)] * 5,
        out_specs=vmem,
        scratch_shapes=[
            pltpu.VMEM((toks, feat), BF16),
            pltpu.VMEM((toks, feat), BF16),
            pltpu.VMEM((toks, feat), BF16),
            pltpu.VMEM((heads, toks), F32),
            pltpu.VMEM(out_weight.shape, BF16),
            pltpu.VMEM((zs, rows, dim), BF16),
            pltpu.VMEM((zs, rows, dim), BF16),
            pltpu.VMEM((heads, 1, dim), F32),
            pltpu.VMEM((zs, 1, dim), F32),
            pltpu.VMEM((zs, rows, dim), F32),
            pltpu.VMEM((zs, 1, dim), F32),
            pltpu.VMEM((rows, dim), BF16),
            pltpu.VMEM((xs, rows, dim), BF16),
            pltpu.VMEM((1, dim), F32),
            pltpu.VMEM((xs, 1, dim), F32),
            pltpu.VMEM((zs, rows, dim), BF16),
            pltpu.VMEM((zs, rows, dim), BF16),
            pltpu.VMEM((toks, feat), F32),
            pltpu.VMEM((toks, heads), F32),
            pltpu.VMEM((toks, feat), BF16),
            pltpu.VMEM((ys, toks, cols), BF16),
            pltpu.VMEM((ys, toks, cols), BF16),
            pltpu.VMEM((ys, toks, cols), BF16),
            pltpu.VMEM((2, toks // 2, cols), BF16),
            pltpu.VMEM((6, toks // 2, cols), BF16),
            dma((zs,)), dma((zs,)), dma((zs,)), dma((zs,)),
            dma((xs,)), dma((xs,)), dma((xs,)), dma((xs,)), dma((zs,)), dma((zs,)),
            dma((ys,)), dma((ys,)), dma((6,)), dma((6,)), dma((5,)),
        ],
        compiler_params=pltpu.CompilerParams(
            collective_id=0, has_side_effects=True, vmem_limit_bytes=60 * 1024 * 1024
        ),
    )(queries, keys, values, log_decay, out_weight)


def solution(mesh, xs=4):
    zs = mesh.shape["seq"] // xs
    ys = mesh.shape["head"] // 2
    return jax.shard_map(
        functools.partial(on_device, xs, zs, ys),
        mesh=mesh,
        in_specs=(
            P("seq", "head"),
            P("seq", "head"),
            P("seq", "head"),
            P("head", "seq"),
            P("head", None),
        ),
        out_specs=P("seq", "head"),
        check_vma=False,
    )
```

```python
import functools

import jax
import jax.numpy as jnp
from jax import lax
from jax.experimental import pallas as pl
from jax.experimental.pallas import tpu as pltpu
from jax.sharding import PartitionSpec as P

MESH = pl.DeviceIdType.MESH
F32, BF16 = jnp.float32, jnp.bfloat16


def far_first(n):
    return sorted(range(1, n), key=lambda k: (-min(k, n - k), k))


def kernel(
    xs, zs, ys,
    q_hbm, k_hbm, v_hbm, g_hbm, w_hbm, out_ref,
    q_ref, k_ref, v_ref, g_ref, w_ref,
    mom_out, mom_in, dec_out, dec_in, pref, pref_decay,
    tot_out, tot_in, end_out, end_in, car_out, car_in,
    intra, grown, normed, pair_out, pair_in, mine, ring_out, ring_in,
    s_mom, r_mom, s_dec, r_dec, s_tot, r_tot, s_end, r_end, s_car, r_car,
    s_pair, r_pair, s_ring, r_ring, s_load,
):
    seq, head = lax.axis_index("seq"), lax.axis_index("head")
    x, z = lax.div(seq, zs), lax.rem(seq, zs)
    y, c = lax.div(head, 2), lax.rem(head, 2)
    heads, toks = g_ref.shape
    dim = q_ref.shape[1] // heads
    rows = heads * dim // zs
    per = dim // rows
    cols = out_ref.shape[1]
    half = toks // 2

    def z_peer(k):
        return (x * zs + lax.rem(z + k, zs), head)

    def x_peer(k):
        return (lax.rem(x + k, xs) * zs + z, head)

    def y_peer(k):
        return (seq, lax.rem(y + k, ys) * 2 + c)

    partner = (seq, y * 2 + 1 - c)

    barrier = pltpu.get_barrier_semaphore()
    peers = [z_peer(k) for k in far_first(zs)] + [x_peer(k) for k in far_first(xs)]
    peers += [partner, y_peer(1), y_peer(ys - 1)]
    for peer in peers:
        pl.semaphore_signal(barrier, inc=1, device_id=peer, device_id_type=MESH)

    loads = []
    for n, (source, target) in enumerate(
        ((g_hbm, g_ref), (k_hbm, k_ref), (v_hbm, v_ref), (q_hbm, q_ref), (w_hbm, w_ref))
    ):
        loads.append(pltpu.make_async_copy(source, target, s_load.at[n]))
        loads[-1].start()

    loads[0].wait()
    g = g_ref[...]
    low = lax.broadcasted_iota(jnp.int32, (toks, toks), 0) >= lax.broadcasted_iota(
        jnp.int32, (toks, toks), 1
    )
    tri = low.astype(F32)
    cum_row = lax.dot_general(
        g, tri, (((1,), (1,)), ((), ())), precision=lax.Precision.HIGHEST,
        preferred_element_type=F32,
    )
    cum_col = cum_row.T
    grown[...] = jnp.exp(cum_col)

    loads[1].wait()
    loads[2].wait()
    for h in range(heads):
        lanes = slice(h * dim, (h + 1) * dim)
        col = cum_col[:, h : h + 1]
        end = cum_col[toks - 1 : toks, h : h + 1]
        scaled = (k_ref[:, lanes].astype(F32) * jnp.exp(end - col)).astype(BF16)
        moments = lax.dot_general(
            scaled, v_ref[:, lanes], (((0,), (0,)), ((), ())), preferred_element_type=F32
        )
        dec_out[h] = jnp.broadcast_to(jnp.exp(end), (1, dim))
        for p in range(per):
            mom_out[h * per + p] = moments[p * rows : (p + 1) * rows].astype(BF16)

    pl.semaphore_wait(barrier, len(peers))

    mom_copies = []
    for k in far_first(zs):
        mom_copies.append(
            pltpu.make_async_remote_copy(
                src_ref=mom_out.at[lax.rem(z + k, zs)], dst_ref=mom_in.at[z],
                send_sem=s_mom.at[k], recv_sem=r_mom.at[k],
                device_id=z_peer(k), device_id_type=MESH,
            )
        )
        mom_copies[-1].start()
        mom_copies.append(
            pltpu.make_async_remote_copy(
                src_ref=dec_out.at[lax.div(lax.rem(z + k, zs), per)], dst_ref=dec_in.at[z],
                send_sem=s_dec.at[k], recv_sem=r_dec.at[k],
                device_id=z_peer(k), device_id_type=MESH,
            )
        )
        mom_copies[-1].start()
    mom_in[z] = mom_out[z]
    dec_in[z] = dec_out[lax.div(z, per)]
    loads[3].wait()

    def within(h):
        lanes = slice(h * dim, (h + 1) * dim)
        scores = lax.dot_general(
            q_ref[:, lanes], k_ref[:, lanes], (((1,), (1,)), ((), ())),
            preferred_element_type=F32,
        )
        gap = cum_col[:, h : h + 1] - cum_row[h : h + 1, :]
        weighted = (scores * jnp.exp(jnp.where(low, gap, -jnp.inf))).astype(BF16)
        intra[:, lanes] = jnp.dot(weighted, v_ref[:, lanes], preferred_element_type=F32)

    for h in range(heads // 2):
        within(h)

    for copy in mom_copies:
        copy.wait_recv()

    state = jnp.zeros((rows, dim), F32)
    decay = jnp.ones((1, dim), F32)
    for j in range(zs):
        pref[j] = state
        pref_decay[j] = decay
        state = state * dec_in[j] + mom_in[j].astype(F32)
        decay = decay * dec_in[j]
    tot_out[...] = state.astype(BF16)
    end_out[...] = decay
    tot_copies = []
    for k in far_first(xs):
        tot_copies.append(
            pltpu.make_async_remote_copy(
                src_ref=tot_out, dst_ref=tot_in.at[x],
                send_sem=s_tot.at[k], recv_sem=r_tot.at[k],
                device_id=x_peer(k), device_id_type=MESH,
            )
        )
        tot_copies[-1].start()
        tot_copies.append(
            pltpu.make_async_remote_copy(
                src_ref=end_out, dst_ref=end_in.at[x],
                send_sem=s_end.at[k], recv_sem=r_end.at[k],
                device_id=x_peer(k), device_id_type=MESH,
            )
        )
        tot_copies[-1].start()
    tot_in[x] = tot_out[...]
    end_in[x] = end_out[...]
    for copy in tot_copies:
        copy.wait_recv()

    before = jnp.zeros((rows, dim), F32)
    for j in range(xs):
        new = before * end_in[j] + tot_in[j].astype(F32)
        before = jnp.where(j < x, new, before)
    for j in range(zs):
        car_out[j] = (pref[j] + pref_decay[j] * before).astype(BF16)
    car_copies = []
    for k in far_first(zs):
        car_copies.append(
            pltpu.make_async_remote_copy(
                src_ref=car_out.at[lax.rem(z + k, zs)], dst_ref=car_in.at[z],
                send_sem=s_car.at[k], recv_sem=r_car.at[k],
                device_id=z_peer(k), device_id_type=MESH,
            )
        )
        car_copies[-1].start()
    car_in[z] = car_out[z]

    for h in range(heads // 2, heads):
        within(h)

    for copy in car_copies:
        copy.wait_recv()

    top, bottom = slice(0, half), slice(half, toks)

    def finish(part):
        for h in range(heads):
            lanes = slice(h * dim, (h + 1) * dim)
            carried = car_in[h * per : (h + 1) * per].reshape(dim, dim)
            inter = jnp.dot(q_ref[part, lanes], carried, preferred_element_type=F32)
            mixed = intra[part, lanes] + inter * grown[part, h : h + 1]
            scale = lax.rsqrt(jnp.mean(mixed * mixed, axis=-1, keepdims=True) + 1e-05)
            normed[part, lanes] = (mixed * scale).astype(BF16)

    def project(to_y, to_c, part):
        start = pl.multiple_of((to_y * 2 + to_c) * cols, 128)
        return jnp.dot(
            normed[part, :], w_ref[:, pl.ds(start, cols)], preferred_element_type=F32
        ).astype(BF16)

    pair_copies = {}

    def give(o, part):
        n, rows_of = part.start // half, pl.ds(part.start, half)
        pair_out[o, part, :] = project(lax.rem(y + o, ys), 1 - c, part)
        pair_copies[o, n] = pltpu.make_async_remote_copy(
            src_ref=pair_out.at[o, rows_of], dst_ref=pair_in.at[o, rows_of],
            send_sem=s_pair.at[2 * o + n], recv_sem=r_pair.at[2 * o + n],
            device_id=partner, device_id_type=MESH,
        )
        pair_copies[o, n].start()

    def keep(o, part):
        own = project(lax.rem(y + o, ys), c, part).astype(F32)
        pair_copies[o, part.start // half].wait_recv()
        mine[o, part, :] = (own + pair_in[o, part, :].astype(F32)).astype(BF16)

    def ring(slot, source, k):
        copy = pltpu.make_async_remote_copy(
            src_ref=source, dst_ref=ring_in.at[slot],
            send_sem=s_ring.at[slot], recv_sem=r_ring.at[slot],
            device_id=y_peer(k), device_id_type=MESH,
        )
        copy.start()
        return copy

    copies = [None] * 6
    finish(top)
    loads[4].wait()
    give(2, top)
    finish(bottom)
    give(2, bottom)
    keep(2, top)
    copies[0] = ring(0, mine.at[2, pl.ds(0, half)], 1)
    give(1, bottom)
    give(3, top)
    keep(2, bottom)
    copies[1] = ring(1, mine.at[2, pl.ds(half, half)], ys - 1)
    keep(1, bottom)
    copies[2] = ring(2, mine.at[1, pl.ds(half, half)], 1)
    keep(3, top)
    copies[3] = ring(3, mine.at[3, pl.ds(0, half)], ys - 1)
    give(1, top)
    give(3, bottom)
    keep(1, top)
    keep(3, bottom)
    copies[0].wait_recv()
    ring_out[0] = (mine[1, top, :].astype(F32) + ring_in[0].astype(F32)).astype(BF16)
    copies[4] = ring(4, ring_out.at[0], 1)
    copies[1].wait_recv()
    ring_out[1] = (mine[3, bottom, :].astype(F32) + ring_in[1].astype(F32)).astype(BF16)
    copies[5] = ring(5, ring_out.at[1], ys - 1)
    for part in (top, bottom):
        give(0, part)
    for part in (top, bottom):
        keep(0, part)
    copies[2].wait_recv()
    mine[0, bottom, :] = (mine[0, bottom, :].astype(F32) + ring_in[2].astype(F32)).astype(BF16)
    copies[3].wait_recv()
    mine[0, top, :] = (mine[0, top, :].astype(F32) + ring_in[3].astype(F32)).astype(BF16)
    copies[4].wait_recv()
    out_ref[top, :] = (mine[0, top, :].astype(F32) + ring_in[4].astype(F32)).astype(BF16)
    copies[5].wait_recv()
    out_ref[bottom, :] = (mine[0, bottom, :].astype(F32) + ring_in[5].astype(F32)).astype(BF16)

    for copy in mom_copies + tot_copies + car_copies + list(pair_copies.values()) + copies:
        copy.wait_send()


def on_device(xs, zs, ys, queries, keys, values, log_decay, out_weight):
    heads, toks = log_decay.shape
    feat = queries.shape[1]
    dim = feat // heads
    rows = feat // zs
    cols = out_weight.shape[1] // (ys * 2)
    vmem = pl.BlockSpec(memory_space=pltpu.VMEM)
    dma = pltpu.SemaphoreType.DMA
    return pl.pallas_call(
        functools.partial(kernel, xs, zs, ys),
        out_shape=jax.ShapeDtypeStruct((toks, cols), BF16),
        in_specs=[pl.BlockSpec(memory_space=pl.ANY)] * 5,
        out_specs=vmem,
        scratch_shapes=[
            pltpu.VMEM((toks, feat), BF16),
            pltpu.VMEM((toks, feat), BF16),
            pltpu.VMEM((toks, feat), BF16),
            pltpu.VMEM((heads, toks), F32),
            pltpu.VMEM(out_weight.shape, BF16),
            pltpu.VMEM((zs, rows, dim), BF16),
            pltpu.VMEM((zs, rows, dim), BF16),
            pltpu.VMEM((heads, 1, dim), F32),
            pltpu.VMEM((zs, 1, dim), F32),
            pltpu.VMEM((zs, rows, dim), F32),
            pltpu.VMEM((zs, 1, dim), F32),
            pltpu.VMEM((rows, dim), BF16),
            pltpu.VMEM((xs, rows, dim), BF16),
            pltpu.VMEM((1, dim), F32),
            pltpu.VMEM((xs, 1, dim), F32),
            pltpu.VMEM((zs, rows, dim), BF16),
            pltpu.VMEM((zs, rows, dim), BF16),
            pltpu.VMEM((toks, feat), F32),
            pltpu.VMEM((toks, heads), F32),
            pltpu.VMEM((toks, feat), BF16),
            pltpu.VMEM((ys, toks, cols), BF16),
            pltpu.VMEM((ys, toks, cols), BF16),
            pltpu.VMEM((ys, toks, cols), BF16),
            pltpu.VMEM((2, toks // 2, cols), BF16),
            pltpu.VMEM((6, toks // 2, cols), BF16),
            dma((zs,)), dma((zs,)), dma((zs,)), dma((zs,)),
            dma((xs,)), dma((xs,)), dma((xs,)), dma((xs,)), dma((zs,)), dma((zs,)),
            dma((2 * ys,)), dma((2 * ys,)), dma((6,)), dma((6,)), dma((5,)),
        ],
        compiler_params=pltpu.CompilerParams(
            collective_id=0, has_side_effects=True, vmem_limit_bytes=60 * 1024 * 1024
        ),
    )(queries, keys, values, log_decay, out_weight)


def solution(mesh, xs=4):
    zs = mesh.shape["seq"] // xs
    ys = mesh.shape["head"] // 2
    return jax.shard_map(
        functools.partial(on_device, xs, zs, ys),
        mesh=mesh,
        in_specs=(
            P("seq", "head"),
            P("seq", "head"),
            P("seq", "head"),
            P("head", "seq"),
            P("head", None),
        ),
        out_specs=P("seq", "head"),
        check_vma=False,
    )
```

```python
import functools

import jax
import jax.numpy as jnp
from jax import lax
from jax.experimental import pallas as pl
from jax.experimental.pallas import tpu as pltpu
from jax.sharding import PartitionSpec as P

MESH = pl.DeviceIdType.MESH
F32, BF16 = jnp.float32, jnp.bfloat16


def far_first(n):
    return sorted(range(1, n), key=lambda k: (-min(k, n - k), k))


def kernel(
    xs, zs, ys,
    q_hbm, k_hbm, v_hbm, g_hbm, w_hbm, out_ref,
    q_ref, k_ref, v_ref, g_ref, w_ref,
    mom_out, mom_in, dec_out, dec_in, pref, pref_decay,
    tot_out, tot_in, end_out, end_in, car_out, car_in,
    intra, grown, normed, pair_out, pair_in, mine, ring_out, ring_in,
    s_mom, r_mom, s_dec, r_dec, s_tot, r_tot, s_end, r_end, s_car, r_car,
    s_pair, r_pair, s_ring, r_ring, s_load,
):
    seq, head = lax.axis_index("seq"), lax.axis_index("head")
    x, z = lax.div(seq, zs), lax.rem(seq, zs)
    y, c = lax.div(head, 2), lax.rem(head, 2)
    heads, toks = g_ref.shape
    dim = q_ref.shape[1] // heads
    rows = heads * dim // zs
    per = dim // rows
    cols = out_ref.shape[1]
    half = toks // 2

    def z_peer(k):
        return (x * zs + lax.rem(z + k, zs), head)

    def x_peer(k):
        return (lax.rem(x + k, xs) * zs + z, head)

    def y_peer(k):
        return (seq, lax.rem(y + k, ys) * 2 + c)

    partner = (seq, y * 2 + 1 - c)

    barrier = pltpu.get_barrier_semaphore()
    peers = [z_peer(k) for k in far_first(zs)] + [x_peer(k) for k in far_first(xs)]
    peers += [partner, y_peer(1), y_peer(ys - 1)]
    for peer in peers:
        pl.semaphore_signal(barrier, inc=1, device_id=peer, device_id_type=MESH)

    loads = []
    for n, (source, target) in enumerate(
        ((g_hbm, g_ref), (k_hbm, k_ref), (v_hbm, v_ref), (q_hbm, q_ref), (w_hbm, w_ref))
    ):
        loads.append(pltpu.make_async_copy(source, target, s_load.at[n]))
        loads[-1].start()

    loads[0].wait()
    g = g_ref[...]
    low = lax.broadcasted_iota(jnp.int32, (toks, toks), 0) >= lax.broadcasted_iota(
        jnp.int32, (toks, toks), 1
    )
    tri = low.astype(F32)
    cum_row = lax.dot_general(
        g, tri, (((1,), (1,)), ((), ())), precision=lax.Precision.HIGHEST,
        preferred_element_type=F32,
    )
    cum_col = cum_row.T
    grown[...] = jnp.exp(cum_col)

    loads[1].wait()
    loads[2].wait()
    for h in range(heads):
        lanes = slice(h * dim, (h + 1) * dim)
        col = cum_col[:, h : h + 1]
        end = cum_col[toks - 1 : toks, h : h + 1]
        scaled = (k_ref[:, lanes].astype(F32) * jnp.exp(end - col)).astype(BF16)
        moments = lax.dot_general(
            scaled, v_ref[:, lanes], (((0,), (0,)), ((), ())), preferred_element_type=F32
        )
        dec_out[h] = jnp.broadcast_to(jnp.exp(end), (1, dim))
        for p in range(per):
            mom_out[h * per + p] = moments[p * rows : (p + 1) * rows].astype(BF16)

    pl.semaphore_wait(barrier, len(peers))

    pieces = [(n, pl.ds(n * (rows // 2), rows // 2)) for n in range(2)]

    def z_copies(source, target, send, recv):
        made = [[], []]
        for n, piece in pieces:
            for k in far_first(zs):
                made[n].append(
                    pltpu.make_async_remote_copy(
                        src_ref=source.at[lax.rem(z + k, zs), piece], dst_ref=target.at[z, piece],
                        send_sem=send.at[n * zs + k], recv_sem=recv.at[n * zs + k],
                        device_id=z_peer(k), device_id_type=MESH,
                    )
                )
        return made

    dec_copies = []
    for k in far_first(zs):
        dec_copies.append(
            pltpu.make_async_remote_copy(
                src_ref=dec_out.at[lax.div(lax.rem(z + k, zs), per)], dst_ref=dec_in.at[z],
                send_sem=s_dec.at[k], recv_sem=r_dec.at[k],
                device_id=z_peer(k), device_id_type=MESH,
            )
        )
        dec_copies[-1].start()
    mom_copies = z_copies(mom_out, mom_in, s_mom, r_mom)
    for copy in mom_copies[0] + mom_copies[1]:
        copy.start()
    mom_in[z] = mom_out[z]
    dec_in[z] = dec_out[lax.div(z, per)]
    loads[3].wait()

    def within(h):
        lanes = slice(h * dim, (h + 1) * dim)
        scores = lax.dot_general(
            q_ref[:, lanes], k_ref[:, lanes], (((1,), (1,)), ((), ())),
            preferred_element_type=F32,
        )
        gap = cum_col[:, h : h + 1] - cum_row[h : h + 1, :]
        weighted = (scores * jnp.exp(jnp.where(low, gap, -jnp.inf))).astype(BF16)
        intra[:, lanes] = jnp.dot(weighted, v_ref[:, lanes], preferred_element_type=F32)

    for h in range(heads // 2):
        within(h)

    for copy in dec_copies:
        copy.wait_recv()
    decay = jnp.ones((1, dim), F32)
    for j in range(zs):
        pref_decay[j] = decay
        decay = decay * dec_in[j]
    end_out[...] = decay
    end_in[x] = decay
    end_copies = []
    for k in far_first(xs):
        end_copies.append(
            pltpu.make_async_remote_copy(
                src_ref=end_out, dst_ref=end_in.at[x],
                send_sem=s_end.at[k], recv_sem=r_end.at[k],
                device_id=x_peer(k), device_id_type=MESH,
            )
        )
        end_copies[-1].start()

    tot_copies = [[], []]
    for n, piece in pieces:
        for copy in mom_copies[n]:
            copy.wait_recv()
        state = jnp.zeros((rows // 2, dim), F32)
        for j in range(zs):
            pref[j, piece, :] = state
            state = state * dec_in[j] + mom_in[j, piece, :].astype(F32)
        tot_out[piece, :] = state.astype(BF16)
        for k in far_first(xs):
            tot_copies[n].append(
                pltpu.make_async_remote_copy(
                    src_ref=tot_out.at[piece], dst_ref=tot_in.at[x, piece],
                    send_sem=s_tot.at[n * xs + k], recv_sem=r_tot.at[n * xs + k],
                    device_id=x_peer(k), device_id_type=MESH,
                )
            )
            tot_copies[n][-1].start()
        tot_in[x, piece, :] = state.astype(BF16)

    for copy in end_copies:
        copy.wait_recv()
    car_copies = z_copies(car_out, car_in, s_car, r_car)
    for n, piece in pieces:
        for copy in tot_copies[n]:
            copy.wait_recv()
        before = jnp.zeros((rows // 2, dim), F32)
        for j in range(xs):
            new = before * end_in[j] + tot_in[j, piece, :].astype(F32)
            before = jnp.where(j < x, new, before)
        for j in range(zs):
            car_out[j, piece, :] = (pref[j, piece, :] + pref_decay[j] * before).astype(BF16)
        for copy in car_copies[n]:
            copy.start()
    car_in[z] = car_out[z]

    for h in range(heads // 2, heads):
        within(h)

    for copy in car_copies[0] + car_copies[1]:
        copy.wait_recv()

    top, bottom = slice(0, half), slice(half, toks)

    def finish(part):
        for h in range(heads):
            lanes = slice(h * dim, (h + 1) * dim)
            carried = car_in[h * per : (h + 1) * per].reshape(dim, dim)
            inter = jnp.dot(q_ref[part, lanes], carried, preferred_element_type=F32)
            mixed = intra[part, lanes] + inter * grown[part, h : h + 1]
            scale = lax.rsqrt(jnp.mean(mixed * mixed, axis=-1, keepdims=True) + 1e-05)
            normed[part, lanes] = (mixed * scale).astype(BF16)

    def project(to_y, to_c, part):
        start = pl.multiple_of((to_y * 2 + to_c) * cols, 128)
        return jnp.dot(
            normed[part, :], w_ref[:, pl.ds(start, cols)], preferred_element_type=F32
        ).astype(BF16)

    pair_copies = {}

    def give(o, part):
        n, rows_of = part.start // half, pl.ds(part.start, half)
        pair_out[o, part, :] = project(lax.rem(y + o, ys), 1 - c, part)
        pair_copies[o, n] = pltpu.make_async_remote_copy(
            src_ref=pair_out.at[o, rows_of], dst_ref=pair_in.at[o, rows_of],
            send_sem=s_pair.at[2 * o + n], recv_sem=r_pair.at[2 * o + n],
            device_id=partner, device_id_type=MESH,
        )
        pair_copies[o, n].start()

    def keep(o, part):
        own = project(lax.rem(y + o, ys), c, part).astype(F32)
        pair_copies[o, part.start // half].wait_recv()
        mine[o, part, :] = (own + pair_in[o, part, :].astype(F32)).astype(BF16)

    def ring(slot, source, k):
        copy = pltpu.make_async_remote_copy(
            src_ref=source, dst_ref=ring_in.at[slot],
            send_sem=s_ring.at[slot], recv_sem=r_ring.at[slot],
            device_id=y_peer(k), device_id_type=MESH,
        )
        copy.start()
        return copy

    copies = [None] * 6
    finish(top)
    loads[4].wait()
    give(2, top)
    finish(bottom)
    give(2, bottom)
    keep(2, top)
    copies[0] = ring(0, mine.at[2, pl.ds(0, half)], 1)
    give(1, bottom)
    give(3, top)
    keep(2, bottom)
    copies[1] = ring(1, mine.at[2, pl.ds(half, half)], ys - 1)
    keep(1, bottom)
    copies[2] = ring(2, mine.at[1, pl.ds(half, half)], 1)
    keep(3, top)
    copies[3] = ring(3, mine.at[3, pl.ds(0, half)], ys - 1)
    give(1, top)
    give(3, bottom)
    keep(1, top)
    keep(3, bottom)
    copies[0].wait_recv()
    ring_out[0] = (mine[1, top, :].astype(F32) + ring_in[0].astype(F32)).astype(BF16)
    copies[4] = ring(4, ring_out.at[0], 1)
    copies[1].wait_recv()
    ring_out[1] = (mine[3, bottom, :].astype(F32) + ring_in[1].astype(F32)).astype(BF16)
    copies[5] = ring(5, ring_out.at[1], ys - 1)
    for part in (top, bottom):
        give(0, part)
    for part in (top, bottom):
        keep(0, part)
    copies[2].wait_recv()
    mine[0, bottom, :] = (mine[0, bottom, :].astype(F32) + ring_in[2].astype(F32)).astype(BF16)
    copies[3].wait_recv()
    mine[0, top, :] = (mine[0, top, :].astype(F32) + ring_in[3].astype(F32)).astype(BF16)
    copies[4].wait_recv()
    out_ref[top, :] = (mine[0, top, :].astype(F32) + ring_in[4].astype(F32)).astype(BF16)
    copies[5].wait_recv()
    out_ref[bottom, :] = (mine[0, bottom, :].astype(F32) + ring_in[5].astype(F32)).astype(BF16)

    sent = dec_copies + end_copies + list(pair_copies.values()) + copies
    for pair in (mom_copies, tot_copies, car_copies):
        sent += pair[0] + pair[1]
    for copy in sent:
        copy.wait_send()


def on_device(xs, zs, ys, queries, keys, values, log_decay, out_weight):
    heads, toks = log_decay.shape
    feat = queries.shape[1]
    dim = feat // heads
    rows = feat // zs
    cols = out_weight.shape[1] // (ys * 2)
    vmem = pl.BlockSpec(memory_space=pltpu.VMEM)
    dma = pltpu.SemaphoreType.DMA
    return pl.pallas_call(
        functools.partial(kernel, xs, zs, ys),
        out_shape=jax.ShapeDtypeStruct((toks, cols), BF16),
        in_specs=[pl.BlockSpec(memory_space=pl.ANY)] * 5,
        out_specs=vmem,
        scratch_shapes=[
            pltpu.VMEM((toks, feat), BF16),
            pltpu.VMEM((toks, feat), BF16),
            pltpu.VMEM((toks, feat), BF16),
            pltpu.VMEM((heads, toks), F32),
            pltpu.VMEM(out_weight.shape, BF16),
            pltpu.VMEM((zs, rows, dim), BF16),
            pltpu.VMEM((zs, rows, dim), BF16),
            pltpu.VMEM((heads, 1, dim), F32),
            pltpu.VMEM((zs, 1, dim), F32),
            pltpu.VMEM((zs, rows, dim), F32),
            pltpu.VMEM((zs, 1, dim), F32),
            pltpu.VMEM((rows, dim), BF16),
            pltpu.VMEM((xs, rows, dim), BF16),
            pltpu.VMEM((1, dim), F32),
            pltpu.VMEM((xs, 1, dim), F32),
            pltpu.VMEM((zs, rows, dim), BF16),
            pltpu.VMEM((zs, rows, dim), BF16),
            pltpu.VMEM((toks, feat), F32),
            pltpu.VMEM((toks, heads), F32),
            pltpu.VMEM((toks, feat), BF16),
            pltpu.VMEM((ys, toks, cols), BF16),
            pltpu.VMEM((ys, toks, cols), BF16),
            pltpu.VMEM((ys, toks, cols), BF16),
            pltpu.VMEM((2, toks // 2, cols), BF16),
            pltpu.VMEM((6, toks // 2, cols), BF16),
            dma((2 * zs,)), dma((2 * zs,)), dma((zs,)), dma((zs,)),
            dma((2 * xs,)), dma((2 * xs,)), dma((xs,)), dma((xs,)), dma((2 * zs,)), dma((2 * zs,)),
            dma((2 * ys,)), dma((2 * ys,)), dma((6,)), dma((6,)), dma((5,)),
        ],
        compiler_params=pltpu.CompilerParams(
            collective_id=0, has_side_effects=True, vmem_limit_bytes=60 * 1024 * 1024
        ),
    )(queries, keys, values, log_decay, out_weight)


def solution(mesh, xs=4):
    zs = mesh.shape["seq"] // xs
    ys = mesh.shape["head"] // 2
    return jax.shard_map(
        functools.partial(on_device, xs, zs, ys),
        mesh=mesh,
        in_specs=(
            P("seq", "head"),
            P("seq", "head"),
            P("seq", "head"),
            P("head", "seq"),
            P("head", None),
        ),
        out_specs=P("seq", "head"),
        check_vma=False,
    )
```

```python
import functools

import jax
import jax.numpy as jnp
from jax import lax
from jax.experimental import pallas as pl
from jax.experimental.pallas import tpu as pltpu
from jax.sharding import PartitionSpec as P

MESH = pl.DeviceIdType.MESH
F32, BF16 = jnp.float32, jnp.bfloat16


def far_first(n):
    return sorted(range(1, n), key=lambda k: (-min(k, n - k), k))


def kernel(
    xs, zs, ys,
    q_hbm, k_hbm, v_hbm, g_hbm, w_hbm, out_ref,
    q_ref, k_ref, v_ref, g_ref, w_ref,
    mom_out, mom_in, dec_out, dec_in, pref, pref_decay,
    tot_out, tot_in, end_out, end_in, car_out, car_in,
    intra, grown, normed, pair_out, pair_in, mine, ring_out, ring_in,
    s_mom, r_mom, s_dec, r_dec, s_tot, r_tot, s_end, r_end, s_car, r_car,
    s_pair, r_pair, s_ring, r_ring, s_load,
):
    seq, head = lax.axis_index("seq"), lax.axis_index("head")
    x, z = lax.div(seq, zs), lax.rem(seq, zs)
    y, c = lax.div(head, 2), lax.rem(head, 2)
    heads, toks = g_ref.shape
    dim = q_ref.shape[1] // heads
    rows = heads * dim // zs
    per = dim // rows
    cols = out_ref.shape[1]
    half = toks // 2

    def z_peer(k):
        return (x * zs + lax.rem(z + k, zs), head)

    def x_peer(k):
        return (lax.rem(x + k, xs) * zs + z, head)

    def y_peer(k):
        return (seq, lax.rem(y + k, ys) * 2 + c)

    partner = (seq, y * 2 + 1 - c)

    barrier = pltpu.get_barrier_semaphore()
    peers = [z_peer(k) for k in far_first(zs)] + [x_peer(k) for k in far_first(xs)]
    peers += [partner, y_peer(1), y_peer(ys - 1)]
    for peer in peers:
        pl.semaphore_signal(barrier, inc=1, device_id=peer, device_id_type=MESH)

    loads = []
    for n, (source, target) in enumerate(
        ((g_hbm, g_ref), (k_hbm, k_ref), (v_hbm, v_ref), (q_hbm, q_ref), (w_hbm, w_ref))
    ):
        loads.append(pltpu.make_async_copy(source, target, s_load.at[n]))
        loads[-1].start()

    loads[0].wait()
    g = g_ref[...]
    low = lax.broadcasted_iota(jnp.int32, (toks, toks), 0) >= lax.broadcasted_iota(
        jnp.int32, (toks, toks), 1
    )
    tri = low.astype(F32)
    cum_row = lax.dot_general(
        g, tri, (((1,), (1,)), ((), ())), precision=lax.Precision.HIGHEST,
        preferred_element_type=F32,
    )
    cum_col = cum_row.T
    grown[...] = jnp.exp(cum_col)

    loads[1].wait()
    loads[2].wait()
    for h in range(heads):
        lanes = slice(h * dim, (h + 1) * dim)
        col = cum_col[:, h : h + 1]
        end = cum_col[toks - 1 : toks, h : h + 1]
        scaled = (k_ref[:, lanes].astype(F32) * jnp.exp(end - col)).astype(BF16)
        moments = lax.dot_general(
            scaled, v_ref[:, lanes], (((0,), (0,)), ((), ())), preferred_element_type=F32
        )
        dec_out[h] = jnp.broadcast_to(jnp.exp(end), (1, dim))
        for p in range(per):
            mom_out[h * per + p] = moments[p * rows : (p + 1) * rows].astype(BF16)

    pl.semaphore_wait(barrier, len(peers))

    mom_copies = []
    for k in far_first(zs):
        mom_copies.append(
            pltpu.make_async_remote_copy(
                src_ref=mom_out.at[lax.rem(z + k, zs)], dst_ref=mom_in.at[z],
                send_sem=s_mom.at[k], recv_sem=r_mom.at[k],
                device_id=z_peer(k), device_id_type=MESH,
            )
        )
        mom_copies[-1].start()
    for k in far_first(zs):
        mom_copies.append(
            pltpu.make_async_remote_copy(
                src_ref=dec_out.at[lax.div(lax.rem(z + k, zs), per)], dst_ref=dec_in.at[z],
                send_sem=s_dec.at[k], recv_sem=r_dec.at[k],
                device_id=z_peer(k), device_id_type=MESH,
            )
        )
        mom_copies[-1].start()
    mom_in[z] = mom_out[z]
    dec_in[z] = dec_out[lax.div(z, per)]
    loads[3].wait()

    def within(h):
        lanes = slice(h * dim, (h + 1) * dim)
        scores = lax.dot_general(
            q_ref[:, lanes], k_ref[:, lanes], (((1,), (1,)), ((), ())),
            preferred_element_type=F32,
        )
        gap = cum_col[:, h : h + 1] - cum_row[h : h + 1, :]
        weighted = (scores * jnp.exp(jnp.where(low, gap, -jnp.inf))).astype(BF16)
        intra[:, lanes] = jnp.dot(weighted, v_ref[:, lanes], preferred_element_type=F32)

    for h in range(heads // 2):
        within(h)

    for copy in mom_copies:
        copy.wait_recv()

    state = jnp.zeros((rows, dim), F32)
    decay = jnp.ones((1, dim), F32)
    for j in range(zs):
        pref[j] = state
        pref_decay[j] = decay
        state = state * dec_in[j] + mom_in[j].astype(F32)
        decay = decay * dec_in[j]
    tot_out[...] = state.astype(BF16)
    end_out[...] = decay
    tot_copies = []
    for k in far_first(xs):
        tot_copies.append(
            pltpu.make_async_remote_copy(
                src_ref=tot_out, dst_ref=tot_in.at[x],
                send_sem=s_tot.at[k], recv_sem=r_tot.at[k],
                device_id=x_peer(k), device_id_type=MESH,
            )
        )
        tot_copies[-1].start()
        tot_copies.append(
            pltpu.make_async_remote_copy(
                src_ref=end_out, dst_ref=end_in.at[x],
                send_sem=s_end.at[k], recv_sem=r_end.at[k],
                device_id=x_peer(k), device_id_type=MESH,
            )
        )
        tot_copies[-1].start()
    tot_in[x] = tot_out[...]
    end_in[x] = end_out[...]
    for copy in tot_copies:
        copy.wait_recv()

    before = jnp.zeros((rows, dim), F32)
    for j in range(xs):
        new = before * end_in[j] + tot_in[j].astype(F32)
        before = jnp.where(j < x, new, before)
    for j in range(zs):
        car_out[j] = (pref[j] + pref_decay[j] * before).astype(BF16)
    car_copies = []
    for k in far_first(zs):
        car_copies.append(
            pltpu.make_async_remote_copy(
                src_ref=car_out.at[lax.rem(z + k, zs)], dst_ref=car_in.at[z],
                send_sem=s_car.at[k], recv_sem=r_car.at[k],
                device_id=z_peer(k), device_id_type=MESH,
            )
        )
        car_copies[-1].start()
    car_in[z] = car_out[z]

    for h in range(heads // 2, heads):
        within(h)

    for copy in car_copies:
        copy.wait_recv()

    top, bottom = slice(0, half), slice(half, toks)

    def finish(part):
        for h in range(heads):
            lanes = slice(h * dim, (h + 1) * dim)
            carried = car_in[h * per : (h + 1) * per].reshape(dim, dim)
            inter = jnp.dot(q_ref[part, lanes], carried, preferred_element_type=F32)
            mixed = intra[part, lanes] + inter * grown[part, h : h + 1]
            scale = lax.rsqrt(jnp.mean(mixed * mixed, axis=-1, keepdims=True) + 1e-05)
            normed[part, lanes] = (mixed * scale).astype(BF16)

    def project(to_y, to_c, part):
        start = pl.multiple_of((to_y * 2 + to_c) * cols, 128)
        return jnp.dot(
            normed[part, :], w_ref[:, pl.ds(start, cols)], preferred_element_type=F32
        ).astype(BF16)

    pair_copies = {}

    def give(o, part):
        n, rows_of = part.start // half, pl.ds(part.start, half)
        pair_out[o, part, :] = project(lax.rem(y + o, ys), 1 - c, part)
        pair_copies[o, n] = pltpu.make_async_remote_copy(
            src_ref=pair_out.at[o, rows_of], dst_ref=pair_in.at[o, rows_of],
            send_sem=s_pair.at[2 * o + n], recv_sem=r_pair.at[2 * o + n],
            device_id=partner, device_id_type=MESH,
        )
        pair_copies[o, n].start()

    def keep(o, part):
        own = project(lax.rem(y + o, ys), c, part).astype(F32)
        pair_copies[o, part.start // half].wait_recv()
        mine[o, part, :] = (own + pair_in[o, part, :].astype(F32)).astype(BF16)

    def ring(slot, source, k):
        copy = pltpu.make_async_remote_copy(
            src_ref=source, dst_ref=ring_in.at[slot],
            send_sem=s_ring.at[slot], recv_sem=r_ring.at[slot],
            device_id=y_peer(k), device_id_type=MESH,
        )
        copy.start()
        return copy

    copies = [None] * 6
    finish(top)
    loads[4].wait()
    give(2, top)
    finish(bottom)
    give(2, bottom)
    keep(2, top)
    copies[0] = ring(0, mine.at[2, pl.ds(0, half)], 1)
    give(1, bottom)
    give(3, top)
    keep(2, bottom)
    copies[1] = ring(1, mine.at[2, pl.ds(half, half)], ys - 1)
    keep(1, bottom)
    copies[2] = ring(2, mine.at[1, pl.ds(half, half)], 1)
    keep(3, top)
    copies[3] = ring(3, mine.at[3, pl.ds(0, half)], ys - 1)
    give(1, top)
    give(3, bottom)
    keep(1, top)
    keep(3, bottom)
    copies[0].wait_recv()
    ring_out[0] = (mine[1, top, :].astype(F32) + ring_in[0].astype(F32)).astype(BF16)
    copies[4] = ring(4, ring_out.at[0], 1)
    copies[1].wait_recv()
    ring_out[1] = (mine[3, bottom, :].astype(F32) + ring_in[1].astype(F32)).astype(BF16)
    copies[5] = ring(5, ring_out.at[1], ys - 1)
    for part in (top, bottom):
        give(0, part)
    for part in (top, bottom):
        keep(0, part)
    copies[2].wait_recv()
    mine[0, bottom, :] = (mine[0, bottom, :].astype(F32) + ring_in[2].astype(F32)).astype(BF16)
    copies[3].wait_recv()
    mine[0, top, :] = (mine[0, top, :].astype(F32) + ring_in[3].astype(F32)).astype(BF16)
    copies[4].wait_recv()
    out_ref[top, :] = (mine[0, top, :].astype(F32) + ring_in[4].astype(F32)).astype(BF16)
    copies[5].wait_recv()
    out_ref[bottom, :] = (mine[0, bottom, :].astype(F32) + ring_in[5].astype(F32)).astype(BF16)

    for copy in mom_copies + tot_copies + car_copies + list(pair_copies.values()) + copies:
        copy.wait_send()


def on_device(xs, zs, ys, queries, keys, values, log_decay, out_weight):
    heads, toks = log_decay.shape
    feat = queries.shape[1]
    dim = feat // heads
    rows = feat // zs
    cols = out_weight.shape[1] // (ys * 2)
    vmem = pl.BlockSpec(memory_space=pltpu.VMEM)
    dma = pltpu.SemaphoreType.DMA
    return pl.pallas_call(
        functools.partial(kernel, xs, zs, ys),
        out_shape=jax.ShapeDtypeStruct((toks, cols), BF16),
        in_specs=[pl.BlockSpec(memory_space=pl.ANY)] * 5,
        out_specs=vmem,
        scratch_shapes=[
            pltpu.VMEM((toks, feat), BF16),
            pltpu.VMEM((toks, feat), BF16),
            pltpu.VMEM((toks, feat), BF16),
            pltpu.VMEM((heads, toks), F32),
            pltpu.VMEM(out_weight.shape, BF16),
            pltpu.VMEM((zs, rows, dim), BF16),
            pltpu.VMEM((zs, rows, dim), BF16),
            pltpu.VMEM((heads, 1, dim), F32),
            pltpu.VMEM((zs, 1, dim), F32),
            pltpu.VMEM((zs, rows, dim), F32),
            pltpu.VMEM((zs, 1, dim), F32),
            pltpu.VMEM((rows, dim), BF16),
            pltpu.VMEM((xs, rows, dim), BF16),
            pltpu.VMEM((1, dim), F32),
            pltpu.VMEM((xs, 1, dim), F32),
            pltpu.VMEM((zs, rows, dim), BF16),
            pltpu.VMEM((zs, rows, dim), BF16),
            pltpu.VMEM((toks, feat), F32),
            pltpu.VMEM((toks, heads), F32),
            pltpu.VMEM((toks, feat), BF16),
            pltpu.VMEM((ys, toks, cols), BF16),
            pltpu.VMEM((ys, toks, cols), BF16),
            pltpu.VMEM((ys, toks, cols), BF16),
            pltpu.VMEM((2, toks // 2, cols), BF16),
            pltpu.VMEM((6, toks // 2, cols), BF16),
            dma((zs,)), dma((zs,)), dma((zs,)), dma((zs,)),
            dma((xs,)), dma((xs,)), dma((xs,)), dma((xs,)), dma((zs,)), dma((zs,)),
            dma((2 * ys,)), dma((2 * ys,)), dma((6,)), dma((6,)), dma((5,)),
        ],
        compiler_params=pltpu.CompilerParams(
            collective_id=0, has_side_effects=True, vmem_limit_bytes=60 * 1024 * 1024
        ),
    )(queries, keys, values, log_decay, out_weight)


def solution(mesh, xs=4):
    zs = mesh.shape["seq"] // xs
    ys = mesh.shape["head"] // 2
    return jax.shard_map(
        functools.partial(on_device, xs, zs, ys),
        mesh=mesh,
        in_specs=(
            P("seq", "head"),
            P("seq", "head"),
            P("seq", "head"),
            P("head", "seq"),
            P("head", None),
        ),
        out_specs=P("seq", "head"),
        check_vma=False,
    )
```
